32 devices in a mesh: grp: 2 (over y), node: 16 (over z, x, core).
Axes of the slice: x: 2, y: 2, z: 4, core: 2. Of those that a mesh axis runs over, the one named last changes fastest.
Arguments:
- tokens: bfloat16 [128, 7168], P(('grp', 'node')), parts along dimension 0, may hold values from -6 to 6
- routes: int32 [128, 2], P(('grp', 'node')), parts along dimension 0, may hold values from 0 to 3, all different within a row; in each aligned block of 4 rows (0 to 3, 4 to 7, ...) at most 4 rows name the same one
- gates: float32 [128, 2], P(('grp', 'node')), parts along dimension 0, may hold values from 0.05 to 1
- norm_gain: bfloat16 [7168], replicated, may hold values from 0.5 to 1.5
- w_gate: bfloat16 [16, 7168, 256], P('node'), may hold values from -0.0625 to 0.0625
- w_up: bfloat16 [16, 7168, 256], P('node'), may hold values from -0.0625 to 0.0625
- w_down: bfloat16 [16, 256, 7168], P('node'), may hold values from -0.1875 to 0.1875
- queries: bfloat16 [32, 128, 576], P(('grp', 'node')), parts along dimension 0, may hold values from -60 to 60
- cache: bfloat16 [32, 1280, 576], P(('grp', 'node')), parts along dimension 0, may hold values from -6 to 6
- lengths: int32 [32], P(('grp', 'node')), parts along dimension 0, may hold values from 1 to 1280, as said below
Outputs:
- moe_out: bfloat16 [128, 7168], P(('grp', 'node')), parts along dimension 0
- attention_out: bfloat16 [32, 65536], P(('grp', 'node')), parts along dimension 0
The draws below stay inside these ranges and needn't reach their ends.
There are 2 independent parts, one for each index of `grp`. The reference program is written for one: setup_inputs(seed, part) draws one part's arguments, and reference() takes and returns one part's arrays. A program takes and returns all parts, laid end to end along the dimension named above; an argument that names none is the same for every part. Nothing has to cross between parts.
Inputs may be any that keep to these rules, and one draw needn't show every extreme that they name: `routes`: each token names 2 different replicas; within the rows of one device no replica is named by more than 4 tokens. `lengths`: some request has all 1280 positions filled.
All inputs are finite; a program needn't handle non-finite values.
Results may differ from the reference program's by a relative error of at most 0.0077.
Values may be sent and summed in bfloat16 or wider, within the bound.
A program may use at most 128 MiB of HBM per device.

```python
import math
import jax
import jax.numpy as jnp
import numpy as np
from jax import lax

D = 7168
FF = 1024
SPLIT = 4
HEADS = 128
LATENT = 576
VALUE_DIM = 512
CACHE = 1280
TOK_DEV = 4
SLOTS = 4
TOP = 2
CAP = 4
TOKENS = 64
ATT_ROWS = 16
N_NODE = 16


def lengths_of(key):
    first_key, second_key = jax.random.split(jax.random.fold_in(key, 17))
    values = jax.random.randint(first_key, (ATT_ROWS,), 1, CACHE + 1)
    where_full = jax.random.randint(second_key, (), 0, ATT_ROWS)
    return (values.at[where_full].set(CACHE).astype(jnp.int32), where_full)


def cache_of(key):
    normal_rows = jax.random.normal(jax.random.fold_in(key, 29), (ATT_ROWS, CACHE, LATENT), jnp.float32)
    return jnp.clip(normal_rows, -6.0, 6.0)


def draw_lengths(key, part):
    return lengths_of(key)[0]


def draw_cache(key, part):
    return cache_of(key).astype(jnp.bfloat16)


def draw_queries(key, part):
    filled, where_full = lengths_of(key)
    stored = cache_of(key).astype(jnp.bfloat16).astype(jnp.float32)
    key_list = jax.random.split(jax.random.fold_in(key, 31), 8)
    drawn_rows = jnp.clip(jax.random.normal(key_list[0], (ATT_ROWS, HEADS, LATENT), jnp.float32), -6.0, 6.0)
    request_pick = jax.random.randint(key_list[1], (ATT_ROWS,), 0, 4) == 0
    request_pick = request_pick.at[where_full].set(True) & (filled >= 2)
    drawn_head = jax.random.randint(key_list[3], (ATT_ROWS, 1), 0, HEADS)
    head_pick = (jax.random.randint(key_list[2], (ATT_ROWS, HEADS), 0, 8) == 0) | (jnp.arange(HEADS, dtype=jnp.int32)[None, :] == drawn_head)
    chosen = request_pick[:, None] & head_pick
    first_pos = jax.random.randint(key_list[4], (ATT_ROWS,), 0, 1 << 30) % filled
    offset_pos = 1 + jax.random.randint(key_list[5], (ATT_ROWS,), 0, 1 << 30) % jnp.maximum(filled - 1, 1)
    second_pos = (first_pos + offset_pos) % filled
    request_ids = jnp.arange(ATT_ROWS, dtype=jnp.int32)
    key_one = stored[request_ids, first_pos]
    key_two = stored[request_ids, second_pos]
    norm_one = jnp.sum(key_one * key_one, axis=-1)[:, None]
    norm_two = jnp.sum(key_two * key_two, axis=-1)[:, None]
    cross_term = jnp.sum(key_one * key_two, axis=-1)[:, None]
    determinant = norm_one * norm_two - cross_term * cross_term
    strength_list = jnp.array([110.0, 230.0, 360.0], jnp.float32)
    strengths = strength_list[jax.random.randint(key_list[6], (ATT_ROWS, HEADS), 0, 3)]
    score_gap = jax.random.uniform(key_list[7], (ATT_ROWS, HEADS), jnp.float32, 1.0, 3.0)
    scale_root = 192.0 ** 0.5
    target_one = strengths * scale_root
    target_two = (strengths - score_gap) * scale_root
    weight_one = (target_one * norm_two - target_two * cross_term) / determinant
    weight_two = (target_two * norm_one - target_one * cross_term) / determinant
    aligned = weight_one[:, :, None] * key_one[:, None, :] + weight_two[:, :, None] * key_two[:, None, :]
    queries_out = jnp.where(chosen[:, :, None], jnp.clip(aligned, -60.0, 60.0), drawn_rows)
    return queries_out.astype(jnp.bfloat16)


def level_of(rng, dims, pieces, least, largest):
    def one(position, blocks):
        heights = jax.random.uniform(jax.random.fold_in(jax.random.fold_in(rng, 6), position), (blocks,), jnp.float32, least / len(pieces), largest / len(pieces))
        return jnp.repeat(jnp.exp(heights), dims[position] // blocks).reshape((-1,) + (1,) * (len(dims) - position - 1))

    loudness = one(*pieces[0])
    for cut in pieces[1:]:
        loudness = loudness * one(*cut)
    return loudness


def deal_out(rng, own, number, rows, amount, top, bound, slope):
    sequence = jax.random.permutation(rng, amount)
    crowded, common = shares(amount, rows * top, bound, slope, True), shares(amount, rows * top, bound, slope, False)
    places = jnp.arange(amount)

    def named(sizes, turn):
        used = int((sizes > 0).sum())
        fixed = max(1, used // 4)
        passed = fixed + (places - fixed + turn * (used - fixed)) % max(1, amount - fixed)
        return jnp.zeros((amount,), jnp.int32).at[sequence[jnp.where(places < fixed, places, passed)]].set(jnp.asarray(sizes, jnp.int32))

    sizes = jnp.where(number % 4 == 0, named(crowded, number // 4), named(common, number - number // 4 - 1))
    mixed = jax.random.permutation(jax.random.fold_in(own, 3), amount)
    giver, receiver = mixed[0:amount // 2 * 2:2], mixed[1:amount // 2 * 2:2]
    margin = jnp.minimum(sizes[giver] - 1, bound - sizes[receiver]) // 2
    margin = jnp.where((giver == sequence[0]) | (receiver == sequence[0]) | (sizes[receiver] == 0), 0, jnp.maximum(margin, 0))
    passed = jax.random.randint(jax.random.fold_in(own, 4), (amount // 2,), 0, 1 << 20) % (margin + 1)
    sizes = sizes.at[giver].add(-passed).at[receiver].add(passed)
    members = jnp.searchsorted(jnp.cumsum(sizes), jnp.arange(rows * top), side="right").astype(jnp.int32)
    grid = members.reshape(top, rows).T
    grid = grid[jax.random.permutation(jax.random.fold_in(own, 1), rows)]
    turn = jax.random.randint(jax.random.fold_in(own, 2), (rows, 1), 0, top)
    return jnp.take_along_axis(grid, (jnp.arange(top)[None, :] + turn) % top, axis=1)


def shares(amount, total, limit, slope, full):
    loads = [(1 << 20) // math.isqrt(grade ** slope) + 1 for grade in range(1, amount + 1)]
    largest = limit if full else min(limit, max(-(-total // amount), total * loads[0] // sum(loads)))
    least = 1 if total - largest >= amount - 1 else 0
    counts, surplus = [largest] + [least] * (amount - 1), total - largest - least * (amount - 1)
    while surplus > 0:
        candidates = [i for i in range(1, amount) if counts[i] < largest] or [i for i in range(1, amount) if counts[i] < limit]
        mass, left = sum([loads[i] for i in candidates]), surplus
        for i in candidates:
            addition = min(limit - counts[i], max(1, left * loads[i] // mass), surplus)
            counts[i] = counts[i] + addition
            surplus = surplus - addition
    return np.array(counts)


def centred(key, dims, width, most, cuts=(), kind=jnp.bfloat16):
    values = jax.random.normal(key, dims, jnp.float32) * width
    if len(cuts) > 0:
        values = level_of(key, dims, cuts, -0.22, 0.18) * values
    return jnp.clip(values, min=-most, max=most).astype(kind)


def setup_inputs(seed: int = 0, part: int = 0) -> dict:
    arg_keys = jax.random.split(jax.random.key(seed), 11)
    own_keys = jax.random.split(jax.random.fold_in(arg_keys[10], part), 11)
    tokens = centred(own_keys[0], (TOKENS, D), 1.0, 6.0, ((0, 16),))
    routes_keys = jax.random.split(jax.random.fold_in(own_keys[1], 1), TOKENS // TOK_DEV)
    routes_turns = jax.random.permutation(jax.random.fold_in(own_keys[1], 3), TOKENS // TOK_DEV)
    routes = jax.vmap(lambda own, number: deal_out(jax.random.fold_in(own_keys[1], 2), own, number, TOK_DEV, SLOTS, TOP, CAP, 2))(routes_keys, routes_turns).reshape((TOKENS, TOP))
    gates = jnp.clip(jnp.exp(math.log(1.0) - 2.9957323 * jax.random.uniform(own_keys[2], (TOKENS, TOP), jnp.float32) ** level_of(own_keys[2], (TOKENS, TOP), ((0, 16),), -0.2, 0.2)), 0.05, 1.0)
    norm_gain = jnp.clip(1.0 + 0.1 * jax.random.normal(arg_keys[3], (D,), jnp.float32), 0.5, 1.5).astype(jnp.bfloat16)
    w_gate = centred(arg_keys[4], (SLOTS * SPLIT, D, FF // SPLIT), D ** -0.5, 0.0625, ((0, 16),))
    w_up = centred(arg_keys[5], (SLOTS * SPLIT, D, FF // SPLIT), D ** -0.5, 0.0625, ((0, 16),))
    w_down = centred(arg_keys[6], (SLOTS * SPLIT, FF // SPLIT, D), FF ** -0.5, 0.1875, ((0, 16),))
    queries = draw_queries(jax.random.fold_in(jax.random.fold_in(arg_keys[10], part), 71), part)
    cache = draw_cache(jax.random.fold_in(jax.random.fold_in(arg_keys[10], part), 71), part)
    lengths = draw_lengths(jax.random.fold_in(jax.random.fold_in(arg_keys[10], part), 71), part)
    return dict(tokens=tokens, routes=routes, gates=gates, norm_gain=norm_gain, w_gate=w_gate, w_up=w_up, w_down=w_down, queries=queries, cache=cache, lengths=lengths)


norm_eps = 1e-06
route_scale = 2.5
softmax_scale = 192.0 ** (-0.5)

def reference(tokens, routes, gates, norm_gain, w_gate, w_up, w_down, queries, cache, lengths):
    hidden_in = tokens.astype(jnp.float32)
    inverse = lax.rsqrt(lax.optimization_barrier(jnp.mean(hidden_in * hidden_in, axis=-1, keepdims=True)) + norm_eps)
    normed = (hidden_in * inverse * norm_gain.astype(jnp.float32)).astype(jnp.bfloat16)
    mixing = route_scale * gates / lax.optimization_barrier(jnp.sum(gates, axis=-1, keepdims=True))
    flat_routes = routes.reshape(-1)
    flat_mixing = mixing.reshape(-1)
    most_rows = N_NODE * CAP

    def one_slot(total, slot_id):
        hits = flat_routes == slot_id
        found = jnp.nonzero(hits, size=most_rows, fill_value=0)[0].astype(jnp.int32)
        valid = jnp.arange(most_rows, dtype=jnp.int32) < jnp.sum(hits.astype(jnp.int32))
        row_ids = found // TOP
        chosen = normed[row_ids]
        summed = jnp.zeros((most_rows, D), jnp.float32)
        for piece in range(SPLIT):
            index = slot_id * SPLIT + piece
            gate_part = jnp.dot(chosen, w_gate[index], preferred_element_type=jnp.float32)
            up_part = jnp.dot(chosen, w_up[index], preferred_element_type=jnp.float32)
            hidden = (jax.nn.silu(gate_part) * up_part).astype(jnp.bfloat16)
            result = jnp.dot(hidden, w_down[index], preferred_element_type=jnp.float32).astype(jnp.bfloat16)
            summed = summed + result.astype(jnp.float32)
        summed_round = lax.optimization_barrier(summed.astype(jnp.bfloat16)).astype(jnp.float32)
        weighted = summed_round * flat_mixing[found][:, None]
        target = jnp.where(valid, row_ids, TOKENS)
        return (total.at[target].add(weighted.astype(total.dtype), mode='drop'), None)
    start = jnp.zeros((TOKENS, D), jnp.float32)
    total, unused = lax.scan(one_slot, start, jnp.arange(SLOTS, dtype=jnp.int32))
    moe_out = total.astype(jnp.bfloat16)

    def one_request(packed):
        query_row, cache_row, filled = packed
        scores = jnp.einsum('hc,jc->hj', query_row.astype(jnp.float32), cache_row.astype(jnp.float32)) * softmax_scale
        valid = jnp.arange(CACHE, dtype=jnp.int32)[None, :] < filled
        scores = jnp.where(valid, scores, -jnp.inf)
        probs = jax.nn.softmax(scores, axis=-1).astype(jnp.bfloat16)
        attended = jnp.dot(probs, cache_row[:, :VALUE_DIM], preferred_element_type=jnp.float32)
        return attended.astype(jnp.bfloat16).reshape(HEADS * VALUE_DIM)
    attention_out = lax.map(one_request, (queries, cache, lengths))
    return (moe_out, attention_out)
```

```python
import functools

import jax
import jax.numpy as jnp
from jax import lax
from jax.experimental import pallas as pl
from jax.experimental.pallas import tpu as pltpu
from jax.sharding import PartitionSpec as P

SPLIT = 4
VALUE_DIM = 512
CHUNKS = 4
BACK_CHUNKS = 4

norm_eps = 1e-06
route_scale = 2.5
softmax_scale = 192.0 ** (-0.5)
MESH = pl.DeviceIdType.MESH
f32 = jnp.float32
bf16 = jnp.bfloat16


def kernel(
    slots,
    tok_ref, gain_ref, routes_ref, gates_ref, len_ref,
    wg_hbm, wu_hbm, wd_hbm, q_hbm, cache_hbm,
    moe_ref, att_hbm,
    wg, wu, wd, qv, cv, av, probs,
    rows, asm32, full, gate_acc, up_acc,
    part, from_core, own32, to_x, from_x, split32, outgoing, back,
    w_sem, l_sem,
    s1_send, s1_recv, c_send, c_recv, x_send, x_recv, f_send, f_recv,
    ra_send, ra_recv, rb_send, rb_recv, rc_send, rc_recv,
):
    node = lax.axis_index("node")
    slot = lax.div(node, SPLIT)
    piece = lax.rem(node, SPLIT)
    core = lax.rem(piece, 2)
    chip = lax.div(piece, 2)
    piece_c = piece + 1 - 2 * core
    piece_x = piece + 2 - 4 * chip
    piece_d = piece_c + 2 - 4 * chip
    node_c = slot * SPLIT + piece_c
    node_x = slot * SPLIT + piece_x
    row_count, width = tok_ref.shape
    cols = width // CHUNKS
    back_cols = width // BACK_CHUNKS
    block = row_count * slots
    others = [lax.rem(slot + step, slots) for step in range(1, slots)]

    def remote(src, dst, send, recv, target):
        return pltpu.make_async_remote_copy(
            src_ref=src, dst_ref=dst, send_sem=send, recv_sem=recv,
            device_id={"node": target}, device_id_type=MESH,
        )

    load_q = pltpu.make_async_copy(q_hbm.at[0], qv, l_sem.at[0])
    load_c = pltpu.make_async_copy(cache_hbm.at[0], cv, l_sem.at[1])
    load_wd = pltpu.make_async_copy(wd_hbm.at[0], wd, l_sem.at[2])
    store_a = pltpu.make_async_copy(av, att_hbm.at[0], l_sem.at[3])
    barrier = pltpu.get_barrier_semaphore()
    for other in others:
        pl.semaphore_signal(barrier, inc=1, device_id={"node": other * SPLIT + piece}, device_id_type=MESH)
    for target in (node_c, node_x):
        pl.semaphore_signal(barrier, inc=1, device_id={"node": target}, device_id_type=MESH)
    load_q.start()
    load_c.start()
    w_loads = []
    for k in range(CHUNKS):
        span = pl.ds(k * cols, cols)
        pair = (
            pltpu.make_async_copy(wg_hbm.at[0, span], wg.at[span], w_sem.at[0, k]),
            pltpu.make_async_copy(wu_hbm.at[0, span], wu.at[span], w_sem.at[1, k]),
        )
        for copy in pair:
            copy.start()
        w_loads.append(pair)
    load_wd.start()

    hidden_in = tok_ref[...].astype(f32)
    inverse = lax.rsqrt(jnp.mean(hidden_in * hidden_in, axis=-1, keepdims=True) + norm_eps)
    normed = (hidden_in * inverse * gain_ref[...].astype(f32)).astype(bf16)
    for k in range(CHUNKS):
        rows[k, slot] = normed[:, k * cols:(k + 1) * cols]
    pl.semaphore_wait(barrier, slots + 1)

    def s1(k, source, target):
        return remote(
            rows.at[k, source], rows.at[k, source],
            s1_send.at[k, target], s1_recv.at[k, source], target * SPLIT + piece,
        )

    for k in range(CHUNKS):
        for other in others:
            s1(k, slot, other).start()

    load_q.wait()
    load_c.wait()
    scores = lax.dot_general(
        qv[...], cv[...], (((1,), (1,)), ((), ())), preferred_element_type=f32
    ) * softmax_scale
    valid = lax.broadcasted_iota(jnp.int32, scores.shape, 1) < len_ref[0]
    scores = jnp.where(valid, scores, -jnp.inf)
    weights = jnp.exp(scores - jnp.max(scores, axis=-1, keepdims=True))
    total = jnp.sum(weights, axis=-1, keepdims=True)
    probs[...] = (weights / total).astype(bf16)

    def to_core(k):
        return remote(full.at[k, piece], full.at[k, piece], c_send.at[k], c_recv.at[k], node_c)

    def to_chip(k):
        return remote(full.at[k, piece], full.at[k, piece], x_send.at[k], x_recv.at[k], node_x)

    def forward(k):
        return remote(full.at[k, piece_x], full.at[k, piece_x], f_send.at[k], f_recv.at[k], node_c)

    def gather(k):
        for other in others:
            s1(k, other, other).wait_recv()
        for s in range(slots):
            asm32[k % 2, pl.ds(s * row_count, row_count), :] = rows[k, s].astype(f32)
        full[k, piece] = asm32[k % 2].astype(bf16)
        to_chip(k).start()
        to_core(k).start()

    def pass_on(k):
        to_chip(k).wait_recv()
        forward(k).start()

    def project(k):
        to_core(k).wait_recv()
        forward(k).wait_recv()
        for copy in w_loads[k]:
            copy.wait()
        x = full[k].reshape(SPLIT * block, cols)
        gate_part = jnp.dot(x, wg[pl.ds(k * cols, cols), :], preferred_element_type=f32)
        up_part = jnp.dot(x, wu[pl.ds(k * cols, cols), :], preferred_element_type=f32)
        if k == 0:
            gate_acc[...] = gate_part
            up_acc[...] = up_part
        else:
            gate_acc[...] += gate_part
            up_acc[...] += up_part

    for k in range(CHUNKS):
        gather(k)
        if k >= 1:
            pass_on(k - 1)
    av[...] = jnp.dot(probs[...], cv[:, :VALUE_DIM], preferred_element_type=f32).astype(bf16)
    store_a.start()
    pass_on(CHUNKS - 1)
    for k in range(CHUNKS):
        project(k)
    gate = gate_acc[...]
    hidden = (gate / (1.0 + jnp.exp(-gate)) * up_acc[...]).astype(bf16)
    load_wd.wait()

    def ra(j):
        return remote(part.at[j, 1 - core], from_core.at[j], ra_send.at[j], ra_recv.at[j], node_c)

    def rb(j):
        return remote(to_x.at[j], from_x.at[j], rb_send.at[j], rb_recv.at[j], node_x)

    def rc(j, origin, target):
        return remote(
            outgoing.at[j, target], back.at[j, origin],
            rc_send.at[j, target], rc_recv.at[j, origin], target * SPLIT + piece,
        )

    def down(j):
        result = jnp.dot(
            hidden, wd[:, pl.ds(j * back_cols, back_cols)], preferred_element_type=f32
        ).astype(bf16)
        for p in range(SPLIT):
            part[j, p % 2, p // 2] = result[p * block:(p + 1) * block]
        ra(j).start()

    def sum_core(j):
        ra(j).wait_recv()
        to_x[j] = (
            part[j, core, 1 - chip].astype(f32) + from_core[j, 1 - chip].astype(f32)
        ).astype(bf16)
        rb(j).start()
        own32[j] = part[j, core, chip].astype(f32) + from_core[j, chip].astype(f32)

    def sum_chip(j):
        rb(j).wait_recv()
        split32[j % 2] = own32[j] + from_x[j].astype(f32)
        for s in range(slots):
            outgoing[j, s] = split32[j % 2, pl.ds(s * row_count, row_count), :].astype(bf16)
        for other in others:
            rc(j, slot, other).start()

    picks = routes_ref[...]
    mixing = gates_ref[...]
    mixing = route_scale * mixing / jnp.sum(mixing, axis=-1, keepdims=True)

    def share(s):
        return jnp.sum(jnp.where(picks == s, mixing, 0.0), axis=-1, keepdims=True)

    def finish(j):
        for other in others:
            rc(j, other, other).wait_recv()
        back[j, slot] = outgoing[j, slot]
        moe = share(0) * back[j, 0].astype(f32)
        for s in range(1, slots):
            moe += share(s) * back[j, s].astype(f32)
        moe_ref[:, pl.ds(j * back_cols, back_cols)] = moe.astype(bf16)

    for j in range(BACK_CHUNKS):
        down(j)
        if j >= 1:
            sum_core(j - 1)
    sum_core(BACK_CHUNKS - 1)
    for j in range(BACK_CHUNKS):
        sum_chip(j)
    for j in range(BACK_CHUNKS):
        finish(j)

    for k in range(CHUNKS):
        for other in others:
            s1(k, slot, other).wait_send()
        to_core(k).wait_send()
        to_chip(k).wait_send()
        forward(k).wait_send()
    for j in range(BACK_CHUNKS):
        ra(j).wait_send()
        rb(j).wait_send()
        for other in others:
            rc(j, slot, other).wait_send()
    store_a.wait()


def per_device(tokens, routes, gates, norm_gain, w_gate, w_up, w_down, queries, cache, lengths):
    slots = lax.axis_size("node") // SPLIT
    row_count, width = tokens.shape
    units = w_gate.shape[2]
    _, heads, latent = queries.shape
    cache_len = cache.shape[1]
    block = row_count * slots
    cols = width // CHUNKS
    back_cols = width // BACK_CHUNKS
    vmem = pl.BlockSpec(memory_space=pltpu.VMEM)
    hbm = pl.BlockSpec(memory_space=pltpu.HBM)
    dma = pltpu.SemaphoreType.DMA
    moe_out, attended = pl.pallas_call(
        functools.partial(kernel, slots),
        out_shape=(
            jax.ShapeDtypeStruct((row_count, width), bf16),
            jax.ShapeDtypeStruct((1, heads, VALUE_DIM), bf16),
        ),
        in_specs=[vmem] * 4 + [pl.BlockSpec(memory_space=pltpu.SMEM)] + [hbm] * 5,
        out_specs=(vmem, hbm),
        scratch_shapes=[
            pltpu.VMEM((width, units), bf16),
            pltpu.VMEM((width, units), bf16),
            pltpu.VMEM((units, width), bf16),
            pltpu.VMEM((heads, latent), bf16),
            pltpu.VMEM((cache_len, latent), bf16),
            pltpu.VMEM((heads, VALUE_DIM), bf16),
            pltpu.VMEM((heads, cache_len), bf16),
            pltpu.VMEM((CHUNKS, slots, row_count, cols), bf16),
            pltpu.VMEM((2, block, cols), f32),
            pltpu.VMEM((CHUNKS, SPLIT, block, cols), bf16),
            pltpu.VMEM((SPLIT * block, units), f32),
            pltpu.VMEM((SPLIT * block, units), f32),
            pltpu.VMEM((BACK_CHUNKS, 2, 2, block, back_cols), bf16),
            pltpu.VMEM((BACK_CHUNKS, 2, block, back_cols), bf16),
            pltpu.VMEM((BACK_CHUNKS, block, back_cols), f32),
            pltpu.VMEM((BACK_CHUNKS, block, back_cols), bf16),
            pltpu.VMEM((BACK_CHUNKS, block, back_cols), bf16),
            pltpu.VMEM((2, block, back_cols), f32),
            pltpu.VMEM((BACK_CHUNKS, slots, row_count, back_cols), bf16),
            pltpu.VMEM((BACK_CHUNKS, slots, row_count, back_cols), bf16),
            dma((2, CHUNKS)),
            dma((4,)),
            dma((CHUNKS, slots)),
            dma((CHUNKS, slots)),
            dma((CHUNKS,)), dma((CHUNKS,)),
            dma((CHUNKS,)), dma((CHUNKS,)),
            dma((CHUNKS,)), dma((CHUNKS,)),
            dma((BACK_CHUNKS,)), dma((BACK_CHUNKS,)),
            dma((BACK_CHUNKS,)), dma((BACK_CHUNKS,)),
            dma((BACK_CHUNKS, slots)), dma((BACK_CHUNKS, slots)),
        ],
        compiler_params=pltpu.CompilerParams(
            collective_id=0, has_side_effects=True, vmem_limit_bytes=58 * 1024 * 1024
        ),
    )(
        tokens, norm_gain.reshape(1, width), routes, gates, lengths,
        w_gate, w_up, w_down, queries, cache,
    )
    return (moe_out, attended.reshape(1, heads * VALUE_DIM))


def solution(mesh):
    in_specs = (
        P(("grp", "node"), None),
        P(("grp", "node"), None),
        P(("grp", "node"), None),
        P(),
        P("node", None, None),
        P("node", None, None),
        P("node", None, None),
        P(("grp", "node"), None, None),
        P(("grp", "node"), None, None),
        P(("grp", "node")),
    )
    out_specs = (P(("grp", "node"), None), P(("grp", "node"), None))
    return jax.shard_map(
        per_device, mesh=mesh, in_specs=in_specs, out_specs=out_specs, check_vma=False
    )
```

```python
import functools

import jax
import jax.numpy as jnp
from jax import lax
from jax.experimental import pallas as pl
from jax.experimental.pallas import tpu as pltpu
from jax.sharding import PartitionSpec as P

SPLIT = 4
VALUE_DIM = 512
CHUNKS = 4
BACK_CHUNKS = 4
LANES = 128

norm_eps = 1e-06
route_scale = 2.5
softmax_scale = 192.0 ** (-0.5)
MESH = pl.DeviceIdType.MESH
f32 = jnp.float32
bf16 = jnp.bfloat16


def kernel(
    slots,
    tok_ref, gain_ref, routes_ref, gates_ref, len_ref,
    wg_hbm, wu_hbm, wd_hbm, q_hbm, cache_hbm,
    moe_ref, att_hbm,
    wg, wu, wd, qv, cv, av, probs,
    rows, asm32, full, gate_acc, up_acc,
    part, from_core, own32, to_x, from_x, split32, outgoing, back,
    w_sem, l_sem,
    s1_send, s1_recv, c_send, c_recv, x_send, x_recv, f_send, f_recv,
    ra_send, ra_recv, rb_send, rb_recv, rc_send, rc_recv,
):
    node = lax.axis_index("node")
    slot = lax.div(node, SPLIT)
    piece = lax.rem(node, SPLIT)
    core = lax.rem(piece, 2)
    chip = lax.div(piece, 2)
    piece_c = piece + 1 - 2 * core
    piece_x = piece + 2 - 4 * chip
    piece_d = piece_c + 2 - 4 * chip
    node_c = slot * SPLIT + piece_c
    node_x = slot * SPLIT + piece_x
    row_count, width = tok_ref.shape
    cols = width // CHUNKS
    back_cols = width // BACK_CHUNKS
    block = row_count * slots
    others = [lax.rem(slot + step, slots) for step in range(1, slots)]

    def remote(src, dst, send, recv, target):
        return pltpu.make_async_remote_copy(
            src_ref=src, dst_ref=dst, send_sem=send, recv_sem=recv,
            device_id={"node": target}, device_id_type=MESH,
        )

    load_q = pltpu.make_async_copy(q_hbm.at[0], qv, l_sem.at[0])
    load_c = pltpu.make_async_copy(cache_hbm.at[0], cv, l_sem.at[1])
    load_wd = pltpu.make_async_copy(wd_hbm.at[0], wd, l_sem.at[2])
    store_a = pltpu.make_async_copy(av, att_hbm.at[0], l_sem.at[3])
    barrier = pltpu.get_barrier_semaphore()
    for other in others:
        pl.semaphore_signal(barrier, inc=1, device_id={"node": other * SPLIT + piece}, device_id_type=MESH)
    for target in (node_c, node_x):
        pl.semaphore_signal(barrier, inc=1, device_id={"node": target}, device_id_type=MESH)
    load_q.start()
    load_c.start()
    w_loads = []
    for k in range(CHUNKS):
        span = pl.ds(k * cols, cols)
        pair = (
            pltpu.make_async_copy(wg_hbm.at[0, span], wg.at[span], w_sem.at[0, k]),
            pltpu.make_async_copy(wu_hbm.at[0, span], wu.at[span], w_sem.at[1, k]),
        )
        for copy in pair:
            copy.start()
        w_loads.append(pair)
    load_wd.start()

    hidden_in = tok_ref[...].astype(f32)
    inverse = lax.rsqrt(jnp.mean(hidden_in * hidden_in, axis=-1, keepdims=True) + norm_eps)
    gain = gain_ref[...].astype(f32)
    for k in range(CHUNKS):
        for lane in range(0, cols, LANES):
            start = k * cols + lane
            here = start // LANES
            rows[k, slot, :, lane:lane + LANES] = (
                hidden_in[:, start:start + LANES] * inverse * gain[here:here + 1]
            ).astype(bf16)
    pl.semaphore_wait(barrier, slots + 1)

    def s1(k, source, target):
        return remote(
            rows.at[k, source], rows.at[k, source],
            s1_send.at[k, target], s1_recv.at[k, source], target * SPLIT + piece,
        )

    for k in range(CHUNKS):
        for other in others:
            s1(k, slot, other).start()

    load_q.wait()
    load_c.wait()
    scores = lax.dot_general(
        qv[...], cv[...], (((0,), (0,)), ((), ())), preferred_element_type=f32
    ) * softmax_scale
    valid = lax.broadcasted_iota(jnp.int32, scores.shape, 1) < len_ref[0]
    scores = jnp.where(valid, scores, -jnp.inf)
    weights = jnp.exp(scores - jnp.max(scores, axis=-1, keepdims=True))
    total = jnp.sum(weights, axis=-1, keepdims=True)
    probs[...] = (weights / total).astype(bf16)

    def to_core(k):
        return remote(full.at[k, piece], full.at[k, piece], c_send.at[k], c_recv.at[k], node_c)

    def to_chip(k):
        return remote(full.at[k, piece], full.at[k, piece], x_send.at[k], x_recv.at[k], node_x)

    def forward(k):
        return remote(full.at[k, piece_x], full.at[k, piece_x], f_send.at[k], f_recv.at[k], node_c)

    def gather(k):
        for other in others:
            s1(k, other, other).wait_recv()
        for s in range(slots):
            asm32[k % 2, pl.ds(s * row_count, row_count), :] = rows[k, s].astype(f32)
        full[k, piece] = asm32[k % 2].astype(bf16)
        to_chip(k).start()
        to_core(k).start()

    def pass_on(k):
        to_chip(k).wait_recv()
        forward(k).start()

    def project(k):
        to_core(k).wait_recv()
        forward(k).wait_recv()
        for copy in w_loads[k]:
            copy.wait()
        x = full[k].reshape(SPLIT * block, cols)
        gate_part = jnp.dot(x, wg[pl.ds(k * cols, cols), :], preferred_element_type=f32)
        up_part = jnp.dot(x, wu[pl.ds(k * cols, cols), :], preferred_element_type=f32)
        if k == 0:
            gate_acc[...] = gate_part
            up_acc[...] = up_part
        else:
            gate_acc[...] += gate_part
            up_acc[...] += up_part

    for k in range(CHUNKS):
        gather(k)
        if k >= 1:
            pass_on(k - 1)
    av[...] = lax.dot_general(
        probs[...], cv[:VALUE_DIM, :], (((1,), (1,)), ((), ())), preferred_element_type=f32
    ).astype(bf16)
    store_a.start()
    pass_on(CHUNKS - 1)
    for k in range(CHUNKS):
        project(k)
    gate = gate_acc[...]
    hidden = (gate / (1.0 + jnp.exp(-gate)) * up_acc[...]).astype(bf16)
    load_wd.wait()

    def ra(j):
        return remote(part.at[j, 1 - core], from_core.at[j], ra_send.at[j], ra_recv.at[j], node_c)

    def rb(j):
        return remote(to_x.at[j], from_x.at[j], rb_send.at[j], rb_recv.at[j], node_x)

    def rc(j, origin, target):
        return remote(
            outgoing.at[j, target], back.at[j, origin],
            rc_send.at[j, target], rc_recv.at[j, origin], target * SPLIT + piece,
        )

    def down(j):
        result = jnp.dot(
            hidden, wd[:, pl.ds(j * back_cols, back_cols)], preferred_element_type=f32
        ).astype(bf16)
        for p in range(SPLIT):
            part[j, p % 2, p // 2] = result[p * block:(p + 1) * block]
        ra(j).start()

    def sum_core(j):
        ra(j).wait_recv()
        to_x[j] = (
            part[j, core, 1 - chip].astype(f32) + from_core[j, 1 - chip].astype(f32)
        ).astype(bf16)
        rb(j).start()
        own32[j] = part[j, core, chip].astype(f32) + from_core[j, chip].astype(f32)

    def sum_chip(j):
        rb(j).wait_recv()
        split32[j % 2] = own32[j] + from_x[j].astype(f32)
        for s in range(slots):
            outgoing[j, s] = split32[j % 2, pl.ds(s * row_count, row_count), :].astype(bf16)
        for other in others:
            rc(j, slot, other).start()

    picks = routes_ref[...]
    mixing = gates_ref[...]
    mixing = route_scale * mixing / jnp.sum(mixing, axis=0, keepdims=True)
    diagonal = (
        lax.broadcasted_iota(jnp.int32, (row_count, row_count), 0)
        == lax.broadcasted_iota(jnp.int32, (row_count, row_count), 1)
    )

    def share(s):
        line = jnp.sum(jnp.where(picks == s, mixing, 0.0), axis=0, keepdims=True)
        line = jnp.broadcast_to(line, (row_count, row_count))
        return jnp.sum(jnp.where(diagonal, line, 0.0), axis=1, keepdims=True)

    shares = [share(s) for s in range(slots)]

    def finish(j):
        for other in others:
            rc(j, other, other).wait_recv()
        back[j, slot] = outgoing[j, slot]
        moe = shares[0] * back[j, 0].astype(f32)
        for s in range(1, slots):
            moe += shares[s] * back[j, s].astype(f32)
        moe_ref[:, pl.ds(j * back_cols, back_cols)] = moe.astype(bf16)

    for j in range(BACK_CHUNKS):
        down(j)
        if j >= 1:
            sum_core(j - 1)
    sum_core(BACK_CHUNKS - 1)
    for j in range(BACK_CHUNKS):
        sum_chip(j)
    for j in range(BACK_CHUNKS):
        finish(j)

    for k in range(CHUNKS):
        for other in others:
            s1(k, slot, other).wait_send()
        to_core(k).wait_send()
        to_chip(k).wait_send()
        forward(k).wait_send()
    for j in range(BACK_CHUNKS):
        ra(j).wait_send()
        rb(j).wait_send()
        for other in others:
            rc(j, slot, other).wait_send()
    store_a.wait()


def per_device(tokens, routes, gates, norm_gain, w_gate, w_up, w_down, queries, cache, lengths):
    slots = lax.axis_size("node") // SPLIT
    row_count, width = tokens.shape
    units = w_gate.shape[2]
    _, heads, latent = queries.shape
    cache_len = cache.shape[1]
    block = row_count * slots
    cols = width // CHUNKS
    back_cols = width // BACK_CHUNKS
    vmem = pl.BlockSpec(memory_space=pltpu.VMEM)
    hbm = pl.BlockSpec(memory_space=pltpu.HBM)
    dma = pltpu.SemaphoreType.DMA
    moe_out, attended = pl.pallas_call(
        functools.partial(kernel, slots),
        out_shape=(
            jax.ShapeDtypeStruct((row_count, width), bf16),
            jax.ShapeDtypeStruct((1, heads, VALUE_DIM), bf16),
        ),
        in_specs=[vmem] * 4 + [pl.BlockSpec(memory_space=pltpu.SMEM)] + [hbm] * 5,
        out_specs=(vmem, hbm),
        scratch_shapes=[
            pltpu.VMEM((width, units), bf16),
            pltpu.VMEM((width, units), bf16),
            pltpu.VMEM((units, width), bf16),
            pltpu.VMEM((latent, heads), bf16),
            pltpu.VMEM((latent, cache_len), bf16),
            pltpu.VMEM((heads, VALUE_DIM), bf16),
            pltpu.VMEM((heads, cache_len), bf16),
            pltpu.VMEM((CHUNKS, slots, row_count, cols), bf16),
            pltpu.VMEM((2, block, cols), f32),
            pltpu.VMEM((CHUNKS, SPLIT, block, cols), bf16),
            pltpu.VMEM((SPLIT * block, units), f32),
            pltpu.VMEM((SPLIT * block, units), f32),
            pltpu.VMEM((BACK_CHUNKS, 2, 2, block, back_cols), bf16),
            pltpu.VMEM((BACK_CHUNKS, 2, block, back_cols), bf16),
            pltpu.VMEM((BACK_CHUNKS, block, back_cols), f32),
            pltpu.VMEM((BACK_CHUNKS, block, back_cols), bf16),
            pltpu.VMEM((BACK_CHUNKS, block, back_cols), bf16),
            pltpu.VMEM((2, block, back_cols), f32),
            pltpu.VMEM((BACK_CHUNKS, slots, row_count, back_cols), bf16),
            pltpu.VMEM((BACK_CHUNKS, slots, row_count, back_cols), bf16),
            dma((2, CHUNKS)),
            dma((4,)),
            dma((CHUNKS, slots)),
            dma((CHUNKS, slots)),
            dma((CHUNKS,)), dma((CHUNKS,)),
            dma((CHUNKS,)), dma((CHUNKS,)),
            dma((CHUNKS,)), dma((CHUNKS,)),
            dma((BACK_CHUNKS,)), dma((BACK_CHUNKS,)),
            dma((BACK_CHUNKS,)), dma((BACK_CHUNKS,)),
            dma((BACK_CHUNKS, slots)), dma((BACK_CHUNKS, slots)),
        ],
        compiler_params=pltpu.CompilerParams(
            collective_id=0, has_side_effects=True, vmem_limit_bytes=58 * 1024 * 1024
        ),
    )(
        tokens, norm_gain.reshape(width // LANES, LANES), routes.T, gates.T, lengths,
        w_gate, w_up, w_down, queries.swapaxes(1, 2), cache.swapaxes(1, 2),
    )
    return (moe_out, attended.reshape(1, heads * VALUE_DIM))


def solution(mesh):
    in_specs = (
        P(("grp", "node"), None),
        P(("grp", "node"), None),
        P(("grp", "node"), None),
        P(),
        P("node", None, None),
        P("node", None, None),
        P("node", None, None),
        P(("grp", "node"), None, None),
        P(("grp", "node"), None, None),
        P(("grp", "node")),
    )
    out_specs = (P(("grp", "node"), None), P(("grp", "node"), None))
    return jax.shard_map(
        per_device, mesh=mesh, in_specs=in_specs, out_specs=out_specs, check_vma=False
    )
```

```python
import functools

import jax
import jax.numpy as jnp
from jax import lax
from jax.experimental import pallas as pl
from jax.experimental.pallas import tpu as pltpu
from jax.sharding import PartitionSpec as P

SPLIT = 4
VALUE_DIM = 512
CHUNKS = 4
BACK_CHUNKS = 2
WINDOW = 3
LANES = 128

norm_eps = 1e-06
route_scale = 2.5
softmax_scale = 192.0 ** (-0.5)
MESH = pl.DeviceIdType.MESH
f32 = jnp.float32
bf16 = jnp.bfloat16


def slot_order(slot, slots):
    if slots & (slots - 1):
        return [lax.rem(slot + step, slots) for step in range(slots)]
    order = [slot]
    bit = 1
    while bit < slots:
        flip = [s + bit - 2 * bit * lax.rem(lax.div(s, bit), 2) for s in order]
        order = order + flip
        bit *= 2
    return order


def kernel(
    slots,
    tok_ref, gain_ref, routes_ref, gates_ref, len_ref,
    wg_hbm, wu_hbm, wd_hbm, q_hbm, cache_hbm,
    moe_ref, att_hbm,
    wg, wu, wd, qv, cv, av, probs,
    rows, asm32, gate_acc, up_acc,
    part, from_core, own32, to_x, from_x, split32, outgoing, back,
    w_sem, l_sem,
    s1_send, s1_recv, c_send, c_recv, x_send, x_recv, f_send, f_recv,
    ra_send, ra_recv, rb_send, rb_recv, rc_send, rc_recv,
):
    node = lax.axis_index("node")
    slot = lax.div(node, SPLIT)
    piece = lax.rem(node, SPLIT)
    core = lax.rem(piece, 2)
    chip = lax.div(piece, 2)
    piece_c = piece + 1 - 2 * core
    piece_x = piece + 2 - 4 * chip
    piece_d = piece_c + 2 - 4 * chip
    node_c = slot * SPLIT + piece_c
    node_x = slot * SPLIT + piece_x
    row_count, width = tok_ref.shape
    cols = width // CHUNKS
    back_cols = width // BACK_CHUNKS
    block = row_count * slots
    order = slot_order(slot, slots)
    others = order[1:]

    def remote(src, dst, send, recv, target):
        return pltpu.make_async_remote_copy(
            src_ref=src, dst_ref=dst, send_sem=send, recv_sem=recv,
            device_id={"node": target}, device_id_type=MESH,
        )

    load_q = pltpu.make_async_copy(q_hbm.at[0], qv, l_sem.at[0])
    load_c = pltpu.make_async_copy(cache_hbm.at[0], cv, l_sem.at[1])
    load_wd = pltpu.make_async_copy(wd_hbm.at[0], wd, l_sem.at[2])
    store_a = pltpu.make_async_copy(av, att_hbm.at[0], l_sem.at[3])
    barrier = pltpu.get_barrier_semaphore()
    for other in others:
        pl.semaphore_signal(barrier, inc=1, device_id={"node": other * SPLIT + piece}, device_id_type=MESH)
    for target in (node_c, node_x):
        pl.semaphore_signal(barrier, inc=1, device_id={"node": target}, device_id_type=MESH)
    load_q.start()
    load_c.start()
    w_loads = []
    for k in range(CHUNKS):
        span = pl.ds(k * cols, cols)
        pair = (
            pltpu.make_async_copy(wg_hbm.at[0, span], wg.at[span], w_sem.at[0, k]),
            pltpu.make_async_copy(wu_hbm.at[0, span], wu.at[span], w_sem.at[1, k]),
        )
        for copy in pair:
            copy.start()
        w_loads.append(pair)
    load_wd.start()

    hidden_in = tok_ref[...].astype(f32)
    inverse = lax.rsqrt(jnp.mean(hidden_in * hidden_in, axis=-1, keepdims=True) + norm_eps)
    gain = gain_ref[...].astype(f32)
    for k in range(CHUNKS):
        for lane in range(0, cols, LANES):
            start = k * cols + lane
            here = start // LANES
            rows[piece, slot, :, start:start + LANES] = (
                hidden_in[:, start:start + LANES] * inverse * gain[here:here + 1]
            ).astype(bf16)
    pl.semaphore_wait(barrier, slots + 1)

    def s1(source, target):
        return remote(
            rows.at[piece, source], rows.at[piece, source],
            s1_send.at[target], s1_recv.at[source], target * SPLIT + piece,
        )

    def to_core(s):
        return remote(rows.at[piece, s], rows.at[piece, s], c_send.at[s], c_recv.at[s], node_c)

    def to_chip(s):
        return remote(rows.at[piece, s], rows.at[piece, s], x_send.at[s], x_recv.at[s], node_x)

    def forward(s):
        return remote(rows.at[piece_x, s], rows.at[piece_x, s], f_send.at[s], f_recv.at[s], node_c)

    for other in others:
        s1(slot, other).start()
    to_chip(slot).start()
    to_core(slot).start()

    load_q.wait()
    load_c.wait()
    scores = lax.dot_general(
        qv[...], cv[...], (((0,), (0,)), ((), ())), preferred_element_type=f32
    ) * softmax_scale
    valid = lax.broadcasted_iota(jnp.int32, scores.shape, 1) < len_ref[0]
    scores = jnp.where(valid, scores, -jnp.inf)
    weights = jnp.exp(scores - jnp.max(scores, axis=-1, keepdims=True))
    total = jnp.sum(weights, axis=-1, keepdims=True)
    probs[...] = (weights / total).astype(bf16)

    for i in range(1, slots):
        s1(order[i], order[i]).wait_recv()
        to_chip(order[i]).start()
        to_core(order[i]).start()
        to_chip(order[i - 1]).wait_recv()
        forward(order[i - 1]).start()
    av[...] = lax.dot_general(
        probs[...], cv[:VALUE_DIM, :], (((1,), (1,)), ((), ())), preferred_element_type=f32
    ).astype(bf16)
    store_a.start()
    to_chip(order[-1]).wait_recv()
    forward(order[-1]).start()
    for s in order:
        to_core(s).wait_recv()
        forward(s).wait_recv()
    for k in range(CHUNKS):
        for p in range(SPLIT):
            for s in range(slots):
                asm32[k % 2, pl.ds((p * slots + s) * row_count, row_count), :] = (
                    rows[p, s, :, pl.ds(k * cols, cols)].astype(f32)
                )
        x = asm32[k % 2].astype(bf16)
        for copy in w_loads[k]:
            copy.wait()
        gate_part = jnp.dot(x, wg[pl.ds(k * cols, cols), :], preferred_element_type=f32)
        up_part = jnp.dot(x, wu[pl.ds(k * cols, cols), :], preferred_element_type=f32)
        if k == 0:
            gate_acc[...] = gate_part
            up_acc[...] = up_part
        else:
            gate_acc[...] += gate_part
            up_acc[...] += up_part
    gate = gate_acc[...]
    hidden = (gate / (1.0 + jnp.exp(-gate)) * up_acc[...]).astype(bf16)
    load_wd.wait()

    def ra(j):
        return remote(part.at[j, 1 - core], from_core.at[j], ra_send.at[j], ra_recv.at[j], node_c)

    def rb(s):
        return remote(to_x.at[s], from_x.at[s], rb_send.at[s], rb_recv.at[s], node_x)

    def rc(origin, target):
        return remote(
            outgoing.at[target], back.at[origin],
            rc_send.at[target], rc_recv.at[origin], target * SPLIT + piece,
        )

    def down(j):
        result = jnp.dot(
            hidden, wd[:, pl.ds(j * back_cols, back_cols)], preferred_element_type=f32
        ).astype(bf16)
        for p in range(SPLIT):
            part[j, p % 2, p // 2] = result[p * block:(p + 1) * block]
        ra(j).start()

    def sum_core(j):
        ra(j).wait_recv()
        span = pl.ds(j * back_cols, back_cols)
        for side, own_side in ((0, 1 - chip), (1, chip)):
            split32[side] = (
                part[j, core, own_side].astype(f32) + from_core[j, own_side].astype(f32)
            )
        for s in range(slots):
            here = pl.ds(s * row_count, row_count)
            to_x[s, :, span] = split32[0, here, :].astype(bf16)
            own32[s, :, span] = split32[1, here, :]

    picks = routes_ref[...]
    mixing = gates_ref[...]
    mixing = route_scale * mixing / jnp.sum(mixing, axis=0, keepdims=True)
    diagonal = (
        lax.broadcasted_iota(jnp.int32, (row_count, row_count), 0)
        == lax.broadcasted_iota(jnp.int32, (row_count, row_count), 1)
    )

    def share(s):
        line = jnp.sum(jnp.where(picks == s, mixing, 0.0), axis=0, keepdims=True)
        line = jnp.broadcast_to(line, (row_count, row_count))
        return jnp.sum(jnp.where(diagonal, line, 0.0), axis=1, keepdims=True)

    shares = [share(s) for s in range(slots)]

    down(0)
    for j in range(BACK_CHUNKS):
        if j + 1 < BACK_CHUNKS:
            down(j + 1)
        sum_core(j)
    home = order[::-1]
    for i in range(min(WINDOW, slots)):
        rb(home[i]).start()
    for i in range(slots):
        s = home[i]
        rb(s).wait_recv()
        if i + WINDOW < slots:
            rb(home[i + WINDOW]).start()
        total_rows = (own32[s] + from_x[s].astype(f32)).astype(bf16)
        if i + 1 < slots:
            outgoing[s] = total_rows
            rc(slot, s).start()
        else:
            back[slot] = total_rows
    for other in others:
        rc(other, other).wait_recv()
    for j in range(BACK_CHUNKS):
        span = pl.ds(j * back_cols, back_cols)
        moe = shares[0] * back[0, :, span].astype(f32)
        for s in range(1, slots):
            moe += shares[s] * back[s, :, span].astype(f32)
        moe_ref[:, span] = moe.astype(bf16)

    for other in others:
        s1(slot, other).wait_send()
        rc(slot, other).wait_send()
    for s in order:
        to_core(s).wait_send()
        to_chip(s).wait_send()
        forward(s).wait_send()
        rb(s).wait_send()
    for j in range(BACK_CHUNKS):
        ra(j).wait_send()
    store_a.wait()


def per_device(tokens, routes, gates, norm_gain, w_gate, w_up, w_down, queries, cache, lengths):
    slots = lax.axis_size("node") // SPLIT
    row_count, width = tokens.shape
    units = w_gate.shape[2]
    _, heads, latent = queries.shape
    cache_len = cache.shape[1]
    block = row_count * slots
    cols = width // CHUNKS
    back_cols = width // BACK_CHUNKS
    vmem = pl.BlockSpec(memory_space=pltpu.VMEM)
    hbm = pl.BlockSpec(memory_space=pltpu.HBM)
    dma = pltpu.SemaphoreType.DMA
    moe_out, attended = pl.pallas_call(
        functools.partial(kernel, slots),
        out_shape=(
            jax.ShapeDtypeStruct((row_count, width), bf16),
            jax.ShapeDtypeStruct((1, heads, VALUE_DIM), bf16),
        ),
        in_specs=[vmem] * 4 + [pl.BlockSpec(memory_space=pltpu.SMEM)] + [hbm] * 5,
        out_specs=(vmem, hbm),
        scratch_shapes=[
            pltpu.VMEM((width, units), bf16),
            pltpu.VMEM((width, units), bf16),
            pltpu.VMEM((units, width), bf16),
            pltpu.VMEM((latent, heads), bf16),
            pltpu.VMEM((latent, cache_len), bf16),
            pltpu.VMEM((heads, VALUE_DIM), bf16),
            pltpu.VMEM((heads, cache_len), bf16),
            pltpu.VMEM((SPLIT, slots, row_count, width), bf16),
            pltpu.VMEM((2, SPLIT * block, cols), f32),
            pltpu.VMEM((SPLIT * block, units), f32),
            pltpu.VMEM((SPLIT * block, units), f32),
            pltpu.VMEM((BACK_CHUNKS, 2, 2, block, back_cols), bf16),
            pltpu.VMEM((BACK_CHUNKS, 2, block, back_cols), bf16),
            pltpu.VMEM((slots, row_count, width), f32),
            pltpu.VMEM((slots, row_count, width), bf16),
            pltpu.VMEM((slots, row_count, width), bf16),
            pltpu.VMEM((2, block, back_cols), f32),
            pltpu.VMEM((slots, row_count, width), bf16),
            pltpu.VMEM((slots, row_count, width), bf16),
            dma((2, CHUNKS)),
            dma((4,)),
            dma((slots,)), dma((slots,)),
            dma((slots,)), dma((slots,)),
            dma((slots,)), dma((slots,)),
            dma((slots,)), dma((slots,)),
            dma((BACK_CHUNKS,)), dma((BACK_CHUNKS,)),
            dma((slots,)), dma((slots,)),
            dma((slots,)), dma((slots,)),
        ],
        compiler_params=pltpu.CompilerParams(
            collective_id=0, has_side_effects=True, vmem_limit_bytes=58 * 1024 * 1024
        ),
    )(
        tokens, norm_gain.reshape(width // LANES, LANES), routes.T, gates.T, lengths,
        w_gate, w_up, w_down, queries.swapaxes(1, 2), cache.swapaxes(1, 2),
    )
    return (moe_out, attended.reshape(1, heads * VALUE_DIM))


def solution(mesh):
    in_specs = (
        P(("grp", "node"), None),
        P(("grp", "node"), None),
        P(("grp", "node"), None),
        P(),
        P("node", None, None),
        P("node", None, None),
        P("node", None, None),
        P(("grp", "node"), None, None),
        P(("grp", "node"), None, None),
        P(("grp", "node")),
    )
    out_specs = (P(("grp", "node"), None), P(("grp", "node"), None))
    return jax.shard_map(
        per_device, mesh=mesh, in_specs=in_specs, out_specs=out_specs, check_vma=False
    )
```

```python
import functools

import jax
import jax.numpy as jnp
from jax import lax
from jax.experimental import pallas as pl
from jax.experimental.pallas import tpu as pltpu
from jax.sharding import PartitionSpec as P

SPLIT = 4
VALUE_DIM = 512
CHUNKS = 4
BACK_CHUNKS = 2
WINDOW = 3
LANES = 128

norm_eps = 1e-06
route_scale = 2.5
softmax_scale = 192.0 ** (-0.5)
MESH = pl.DeviceIdType.MESH
f32 = jnp.float32
bf16 = jnp.bfloat16


def slot_order(slot, slots):
    if slots & (slots - 1):
        return [lax.rem(slot + step, slots) for step in range(slots)]
    order = [slot]
    bit = 1
    while bit < slots:
        flip = [s + bit - 2 * bit * lax.rem(lax.div(s, bit), 2) for s in order]
        order = order + flip
        bit *= 2
    return order


def kernel(
    slots,
    tok_ref, gain_ref, routes_ref, gates_ref, len_ref,
    wg_hbm, wu_hbm, wd_hbm, q_hbm, cache_hbm,
    moe_ref, att_hbm,
    wg, wu, wd, qv, cv, av, probs,
    rows, asm32, gate_acc, up_acc,
    part, from_core, own32, to_x, from_x, split32, outgoing, back,
    w_sem, l_sem,
    s1_send, s1_recv, c_send, c_recv, x_send, x_recv, f_send, f_recv,
    ra_send, ra_recv, rb_send, rb_recv, rc_send, rc_recv,
):
    node = lax.axis_index("node")
    slot = lax.div(node, SPLIT)
    piece = lax.rem(node, SPLIT)
    core = lax.rem(piece, 2)
    chip = lax.div(piece, 2)
    piece_c = piece + 1 - 2 * core
    piece_x = piece + 2 - 4 * chip
    piece_d = piece_c + 2 - 4 * chip
    node_c = slot * SPLIT + piece_c
    node_x = slot * SPLIT + piece_x
    row_count, width = tok_ref.shape
    cols = width // CHUNKS
    back_cols = width // BACK_CHUNKS
    block = row_count * slots
    order = slot_order(slot, slots)
    others = order[1:]

    def remote(src, dst, send, recv, target):
        return pltpu.make_async_remote_copy(
            src_ref=src, dst_ref=dst, send_sem=send, recv_sem=recv,
            device_id={"node": target}, device_id_type=MESH,
        )

    load_q = pltpu.make_async_copy(q_hbm.at[0], qv, l_sem.at[0])
    load_c = pltpu.make_async_copy(cache_hbm.at[0], cv, l_sem.at[1])
    load_wd = pltpu.make_async_copy(wd_hbm.at[0], wd, l_sem.at[2])
    store_a = pltpu.make_async_copy(av, att_hbm.at[0], l_sem.at[3])
    barrier = pltpu.get_barrier_semaphore()
    for other in others:
        pl.semaphore_signal(barrier, inc=1, device_id={"node": other * SPLIT + piece}, device_id_type=MESH)
    for target in (node_c, node_x):
        pl.semaphore_signal(barrier, inc=1, device_id={"node": target}, device_id_type=MESH)
    load_q.start()
    load_c.start()
    w_loads = []
    for k in range(CHUNKS):
        span = pl.ds(k * cols, cols)
        pair = (
            pltpu.make_async_copy(wg_hbm.at[0, span], wg.at[span], w_sem.at[0, k]),
            pltpu.make_async_copy(wu_hbm.at[0, span], wu.at[span], w_sem.at[1, k]),
        )
        for copy in pair:
            copy.start()
        w_loads.append(pair)
    load_wd.start()

    hidden_in = tok_ref[...].astype(f32)
    inverse = lax.rsqrt(jnp.mean(hidden_in * hidden_in, axis=-1, keepdims=True) + norm_eps)
    gain = gain_ref[...].astype(f32)
    for k in range(CHUNKS):
        for lane in range(0, cols, LANES):
            start = k * cols + lane
            here = start // LANES
            rows[piece, slot, :, start:start + LANES] = (
                hidden_in[:, start:start + LANES] * inverse * gain[here:here + 1]
            ).astype(bf16)
    pl.semaphore_wait(barrier, slots + 1)

    def s1(source, target):
        return remote(
            rows.at[piece, source], rows.at[piece, source],
            s1_send.at[target], s1_recv.at[source], target * SPLIT + piece,
        )

    def to_core(s):
        return remote(rows.at[piece, s], rows.at[piece, s], c_send.at[s], c_recv.at[s], node_c)

    def to_chip(s):
        return remote(rows.at[piece, s], rows.at[piece, s], x_send.at[s], x_recv.at[s], node_x)

    def forward(s):
        return remote(rows.at[piece_x, s], rows.at[piece_x, s], f_send.at[s], f_recv.at[s], node_c)

    for other in others:
        s1(slot, other).start()
    to_chip(slot).start()
    to_core(slot).start()

    load_q.wait()
    load_c.wait()
    scores = lax.dot_general(
        qv[...], cv[...], (((0,), (0,)), ((), ())), preferred_element_type=f32
    ) * softmax_scale
    valid = lax.broadcasted_iota(jnp.int32, scores.shape, 1) < len_ref[0]
    scores = jnp.where(valid, scores, -jnp.inf)
    weights = jnp.exp(scores - jnp.max(scores, axis=-1, keepdims=True))
    total = jnp.sum(weights, axis=-1, keepdims=True)
    probs[...] = (weights / total).astype(bf16)

    for i in range(1, slots):
        s1(order[i], order[i]).wait_recv()
        to_chip(order[i]).start()
        to_core(order[i]).start()
        to_chip(order[i - 1]).wait_recv()
        forward(order[i - 1]).start()
    av[...] = lax.dot_general(
        probs[...], cv[:VALUE_DIM, :], (((1,), (1,)), ((), ())), preferred_element_type=f32
    ).astype(bf16)
    store_a.start()
    to_chip(order[-1]).wait_recv()
    forward(order[-1]).start()
    for s in order:
        to_core(s).wait_recv()
        forward(s).wait_recv()
    for k in range(CHUNKS):
        for p in range(SPLIT):
            for s in range(slots):
                asm32[k % 2, pl.ds((p * slots + s) * row_count, row_count), :] = (
                    rows[p, s, :, pl.ds(k * cols, cols)].astype(f32)
                )
        x = asm32[k % 2].astype(bf16)
        for copy in w_loads[k]:
            copy.wait()
        gate_part = jnp.dot(x, wg[pl.ds(k * cols, cols), :], preferred_element_type=f32)
        up_part = jnp.dot(x, wu[pl.ds(k * cols, cols), :], preferred_element_type=f32)
        if k == 0:
            gate_acc[...] = gate_part
            up_acc[...] = up_part
        else:
            gate_acc[...] += gate_part
            up_acc[...] += up_part
    gate = gate_acc[...]
    hidden = (gate / (1.0 + jnp.exp(-gate)) * up_acc[...]).astype(bf16)
    load_wd.wait()

    def ra(j):
        return remote(part.at[j, 1 - core], from_core.at[j], ra_send.at[j], ra_recv.at[j], node_c)

    def rb(s):
        return remote(to_x.at[s], from_x.at[s], rb_send.at[s], rb_recv.at[s], node_x)

    def rc(origin, target):
        return remote(
            outgoing.at[target], back.at[origin],
            rc_send.at[target], rc_recv.at[origin], target * SPLIT + piece,
        )

    def down(j):
        result = jnp.dot(
            hidden, wd[:, pl.ds(j * back_cols, back_cols)], preferred_element_type=f32
        ).astype(bf16)
        for p in range(SPLIT):
            part[j, p % 2, p // 2] = result[p * block:(p + 1) * block]
        ra(j).start()

    def sum_core(j, side, own_side, kept):
        span = pl.ds(j * back_cols, back_cols)
        split32[side] = part[j, core, own_side].astype(f32) + from_core[j, own_side].astype(f32)
        for s in range(slots):
            here = pl.ds(s * row_count, row_count)
            kept[s, :, span] = split32[side, here, :].astype(kept.dtype)

    picks = routes_ref[...]
    mixing = gates_ref[...]
    mixing = route_scale * mixing / jnp.sum(mixing, axis=0, keepdims=True)
    diagonal = (
        lax.broadcasted_iota(jnp.int32, (row_count, row_count), 0)
        == lax.broadcasted_iota(jnp.int32, (row_count, row_count), 1)
    )

    def share(s):
        line = jnp.sum(jnp.where(picks == s, mixing, 0.0), axis=0, keepdims=True)
        line = jnp.broadcast_to(line, (row_count, row_count))
        return jnp.sum(jnp.where(diagonal, line, 0.0), axis=1, keepdims=True)

    shares = [share(s) for s in range(slots)]

    down(0)
    for j in range(BACK_CHUNKS):
        if j + 1 < BACK_CHUNKS:
            down(j + 1)
        ra(j).wait_recv()
        sum_core(j, 0, 1 - chip, to_x)
    home = order[::-1]
    for i in range(min(WINDOW, slots)):
        rb(home[i]).start()
    for j in range(BACK_CHUNKS):
        sum_core(j, 1, chip, own32)
    for i in range(slots):
        s = home[i]
        rb(s).wait_recv()
        if i + WINDOW < slots:
            rb(home[i + WINDOW]).start()
        total_rows = (own32[s] + from_x[s].astype(f32)).astype(bf16)
        if i + 1 < slots:
            outgoing[s] = total_rows
            rc(slot, s).start()
        else:
            back[slot] = total_rows
    for other in others:
        rc(other, other).wait_recv()
    for j in range(BACK_CHUNKS):
        span = pl.ds(j * back_cols, back_cols)
        moe = shares[0] * back[0, :, span].astype(f32)
        for s in range(1, slots):
            moe += shares[s] * back[s, :, span].astype(f32)
        moe_ref[:, span] = moe.astype(bf16)

    for other in others:
        s1(slot, other).wait_send()
        rc(slot, other).wait_send()
    for s in order:
        to_core(s).wait_send()
        to_chip(s).wait_send()
        forward(s).wait_send()
        rb(s).wait_send()
    for j in range(BACK_CHUNKS):
        ra(j).wait_send()
    store_a.wait()


def per_device(tokens, routes, gates, norm_gain, w_gate, w_up, w_down, queries, cache, lengths):
    slots = lax.axis_size("node") // SPLIT
    row_count, width = tokens.shape
    units = w_gate.shape[2]
    _, heads, latent = queries.shape
    cache_len = cache.shape[1]
    block = row_count * slots
    cols = width // CHUNKS
    back_cols = width // BACK_CHUNKS
    vmem = pl.BlockSpec(memory_space=pltpu.VMEM)
    hbm = pl.BlockSpec(memory_space=pltpu.HBM)
    dma = pltpu.SemaphoreType.DMA
    moe_out, attended = pl.pallas_call(
        functools.partial(kernel, slots),
        out_shape=(
            jax.ShapeDtypeStruct((row_count, width), bf16),
            jax.ShapeDtypeStruct((1, heads, VALUE_DIM), bf16),
        ),
        in_specs=[vmem] * 4 + [pl.BlockSpec(memory_space=pltpu.SMEM)] + [hbm] * 5,
        out_specs=(vmem, hbm),
        scratch_shapes=[
            pltpu.VMEM((width, units), bf16),
            pltpu.VMEM((width, units), bf16),
            pltpu.VMEM((units, width), bf16),
            pltpu.VMEM((latent, heads), bf16),
            pltpu.VMEM((latent, cache_len), bf16),
            pltpu.VMEM((heads, VALUE_DIM), bf16),
            pltpu.VMEM((heads, cache_len), bf16),
            pltpu.VMEM((SPLIT, slots, row_count, width), bf16),
            pltpu.VMEM((2, SPLIT * block, cols), f32),
            pltpu.VMEM((SPLIT * block, units), f32),
            pltpu.VMEM((SPLIT * block, units), f32),
            pltpu.VMEM((BACK_CHUNKS, 2, 2, block, back_cols), bf16),
            pltpu.VMEM((BACK_CHUNKS, 2, block, back_cols), bf16),
            pltpu.VMEM((slots, row_count, width), f32),
            pltpu.VMEM((slots, row_count, width), bf16),
            pltpu.VMEM((slots, row_count, width), bf16),
            pltpu.VMEM((2, block, back_cols), f32),
            pltpu.VMEM((slots, row_count, width), bf16),
            pltpu.VMEM((slots, row_count, width), bf16),
            dma((2, CHUNKS)),
            dma((4,)),
            dma((slots,)), dma((slots,)),
            dma((slots,)), dma((slots,)),
            dma((slots,)), dma((slots,)),
            dma((slots,)), dma((slots,)),
            dma((BACK_CHUNKS,)), dma((BACK_CHUNKS,)),
            dma((slots,)), dma((slots,)),
            dma((slots,)), dma((slots,)),
        ],
        compiler_params=pltpu.CompilerParams(
            collective_id=0, has_side_effects=True, vmem_limit_bytes=58 * 1024 * 1024
        ),
    )(
        tokens, norm_gain.reshape(width // LANES, LANES), routes.T, gates.T, lengths,
        w_gate, w_up, w_down, queries.swapaxes(1, 2), cache.swapaxes(1, 2),
    )
    return (moe_out, attended.reshape(1, heads * VALUE_DIM))


def solution(mesh):
    in_specs = (
        P(("grp", "node"), None),
        P(("grp", "node"), None),
        P(("grp", "node"), None),
        P(),
        P("node", None, None),
        P("node", None, None),
        P("node", None, None),
        P(("grp", "node"), None, None),
        P(("grp", "node"), None, None),
        P(("grp", "node")),
    )
    out_specs = (P(("grp", "node"), None), P(("grp", "node"), None))
    return jax.shard_map(
        per_device, mesh=mesh, in_specs=in_specs, out_specs=out_specs, check_vma=False
    )
```
